32 devices in a mesh: dp: 4 (over z), group: 8 (over y, x, core).
Axes of the slice: x: 2, y: 2, z: 4, core: 2. Of those that a mesh axis runs over, the one named last changes fastest.
Arguments:
- tokens: bfloat16 [4096, 1536], P(('dp', 'group')), may hold values from -6 to 6
- grad_out: bfloat16 [4096, 1536], P(('dp', 'group')), may hold values from -6 to 6
- lengths: int32 [32, 3], P(('dp', 'group')), may hold values from 1 to 96, 128 in all within a row
- adapter_ids: int32 [32, 3], P(('dp', 'group')), may hold values from 0 to 7
- dispatch: int32 [4096, 2], P(('dp', 'group')), may hold values from 0 to 255, as said below
- norm_first: bfloat16 [1536], replicated, may hold values from 0.5 to 1.5
- norm_second: bfloat16 [1536], replicated, may hold values from 0.5 to 1.5
- w_qkv: bfloat16 [1536, 2560], P('group'), may hold values from -0.15625 to 0.15625
- w_out: bfloat16 [1536, 1536], P('group'), may hold values from -0.625 to 0.625
- w_router: bfloat16 [1536, 16], replicated, may hold values from -0.078125 to 0.078125
- w_gate_up: bfloat16 [16, 1536, 2048], P('group'), may hold values from -0.15625 to 0.15625
- w_down: bfloat16 [16, 1024, 1536], P('group'), may hold values from -0.375 to 0.375
- qkv_down: bfloat16 [8, 1536, 48], P('group'), may hold values from -0.15625 to 0.15625
- qkv_up: bfloat16 [8, 16, 2560], P('group'), may hold values from -0.75 to 0.75
- out_down: bfloat16 [8, 1536, 16], P('group'), may hold values from -0.15625 to 0.15625
- out_up: bfloat16 [8, 16, 1536], P('group'), may hold values from -3 to 3
- router_down: bfloat16 [8, 1536, 16], P('group'), may hold values from -0.15625 to 0.15625
- router_up: bfloat16 [8, 16, 16], P('group'), may hold values from -0.75 to 0.75
- gu_down: bfloat16 [16, 8, 1536, 32], P('group'), may hold values from -0.15625 to 0.15625
- gu_up: bfloat16 [16, 8, 16, 2048], P('group'), may hold values from -0.75 to 0.75
- dn_down: bfloat16 [16, 8, 1024, 16], P('group'), may hold values from -0.1875 to 0.1875
- dn_up: bfloat16 [16, 8, 16, 1536], P('group'), may hold values from -1.5 to 1.5
Outputs:
- block_out: bfloat16 [4096, 1536], P(('dp', 'group'))
- grad_tokens: float32 [4096, 1536], P(('dp', 'group'))
- grad_qkv_down: float32 [8, 1536, 48], P('group')
- grad_qkv_up: float32 [8, 16, 2560], P('group')
- grad_out_down: float32 [8, 1536, 16], P('group')
- grad_out_up: float32 [8, 16, 1536], P('group')
- grad_router_down: float32 [8, 1536, 16], P('group')
- grad_router_up: float32 [8, 16, 16], P('group')
- grad_gu_down: float32 [16, 8, 1536, 32], P('group')
- grad_gu_up: float32 [16, 8, 16, 2048], P('group')
- grad_dn_down: float32 [16, 8, 1024, 16], P('group')
- grad_dn_up: float32 [16, 8, 16, 1536], P('group')
The draws below stay inside these ranges and needn't reach their ends.
Inputs may be any that keep to these rules, and one draw needn't show every extreme that they name: `lengths`: each device's 3 sequences fill its 128 rows in order; on every device the longest has exactly 96 rows. `dispatch`: on the rows of one device the 256 entries are a permutation of 0 to 255, so that every device receives exactly 8 copies from every device, the first 4 for its first expert and so on; the two copies of a token name different experts.
All inputs are finite; a program needn't handle non-finite values.
Results may differ from the reference program's by a relative error of at most 0.022.
Values may be sent and summed in bfloat16 or wider, within the bound.
No kernel may reach another device: no remote copies, remote signals or barrier semaphores. Data moves between devices by JAX's collectives and lax.ppermute only.
A program may use at most 128 MiB of HBM per device.

```python
import math
import jax
import jax.numpy as jnp
import numpy as np
from jax import lax

D = 1536
QUERY_HEADS = 24
KEY_VALUE_HEADS = 8
HEAD_SIZE = 64
FF = 1024
R = 16
SETS = 8
EXP_DEV = 2
SEQ_DEV = 3
TOK_DEV = 128
LONGEST = 96
QWIDTH = 1536
QKV = 2560
EXPERTS = 16
TOKENS = 4096
PEER_ROWS = 8
N_GROUP = 8
DEVICES = 32


def dispatch_block(device_key):
    key_order, key_within, key_tokens = jax.random.split(device_key, 3)
    per_expert = 2 * TOK_DEV // EXPERTS
    per_slot = PEER_ROWS // EXP_DEV
    expert_order = jax.random.permutation(key_order, EXPERTS).astype(jnp.int32)
    scores = jax.random.randint(key_within, (EXPERTS, per_expert), 0, 2 ** 20) * per_expert + jnp.arange(per_expert, dtype=jnp.int32)[None, :]
    within = jnp.argsort(scores, axis=1).astype(jnp.int32)
    expert = jnp.broadcast_to(expert_order[:, None], (EXPERTS, per_expert))
    replica = within // per_slot
    offset = within % per_slot
    slot_index = (replica * N_GROUP + expert // EXP_DEV) * PEER_ROWS + expert % EXP_DEV * per_slot + offset
    listing = slot_index.reshape(-1).astype(jnp.int32)
    shuffle = jax.random.permutation(key_tokens, TOK_DEV).astype(jnp.int32)
    result = jnp.zeros((TOK_DEV, 2), jnp.int32)
    result = result.at[shuffle, 0].set(listing[:TOK_DEV])
    result = result.at[shuffle, 1].set(listing[TOK_DEV:])
    return result


def draw_dispatch(key, part):
    device_keys = jax.random.split(jax.random.fold_in(key, 17), DEVICES)
    return jax.vmap(dispatch_block)(device_keys).reshape(TOKENS, 2)


def place_ends(entries, rng, low, high):
    dims = entries.shape
    index_at = [jax.random.randint(jax.random.fold_in(rng, axis), (), 0, dims[axis]) for axis in range(len(dims))]
    entries = entries.at[tuple(index_at)].set(low)
    longest = dims.index(max(dims))
    index_at[longest] = (index_at[longest] + 1) % dims[longest]
    return entries.at[tuple(index_at)].set(high)


def steps_of(own_key, dims, shards, smallest, largest):
    gain, own = 1.0, jax.random.fold_in(own_key, 6)
    for axis_at, parts in shards:
        steps = jnp.exp(jax.random.uniform(jax.random.fold_in(own, axis_at), (parts,), jnp.float32, smallest / len(shards), largest / len(shards)))
        gain = gain * jnp.repeat(steps, dims[axis_at] // parts).reshape([-1 if axis == axis_at else 1 for axis in range(len(dims))])
    return gain


def split_up(number_of, total, limit, lean):
    loads = [(1 << 20) // math.isqrt(grade ** lean) + 1 for grade in range(2, number_of + 1)]
    spare, counts = total - limit - (number_of - 1), [1] * (number_of - 1)
    while spare > 0:
        movable = [i for i in range(number_of - 1) if counts[i] < limit]
        whole, remaining = sum([loads[i] for i in movable]), spare
        for i in movable:
            addition = min(limit - counts[i], max(1, remaining * loads[i] // whole), spare)
            counts[i] = counts[i] + addition
            spare = spare - addition
    return np.array([limit] + counts)


def uneven_parts(stream_key, amount, total, bound, lean):
    if amount == 2:
        one = jax.random.randint(stream_key, (), max(1, total - bound), min(bound, total - 1) + 1)
        return jnp.stack([one, total - one])
    tallies = jnp.asarray(split_up(amount, total, bound, lean), jnp.int32)
    twos = (amount - 1) // 2
    donor, receiver = tallies[1:1 + 2 * twos:2], tallies[2:2 + 2 * twos:2]
    room = jnp.minimum(donor - 1, bound - receiver)
    moved = jax.random.randint(jax.random.fold_in(stream_key, 1), (twos,), 0, 1 << 20) % (room + 1)
    tallies = tallies.at[1:1 + 2 * twos:2].set(donor - moved).at[2:2 + 2 * twos:2].set(receiver + moved)
    return tallies[jax.random.permutation(jax.random.fold_in(stream_key, 2), amount)]


def bell_draw(own_key, dims, scale, limit, pieces=(), kind=jnp.bfloat16):
    loudness = steps_of(own_key, dims, pieces, -0.22, 0.18) if pieces else 1.0
    entries = jax.random.normal(own_key, dims, jnp.float32) * scale * loudness
    return jnp.minimum(jnp.maximum(entries, -limit), limit).astype(kind)


def setup_inputs(seed: int = 0) -> dict:
    keys = jax.random.split(jax.random.key(seed), 23)
    return {
        "tokens": bell_draw(keys[0], (TOKENS, D), 1.0, 6.0, ((0, 32),)),
        "grad_out": bell_draw(keys[1], (TOKENS, D), 1.0, 6.0, ((0, 32),)),
        "lengths": jax.vmap(lambda own: uneven_parts(own, SEQ_DEV, TOK_DEV, LONGEST, 1))(jax.random.split(keys[2], DEVICES)).reshape((DEVICES, SEQ_DEV)).astype(jnp.int32),
        "adapter_ids": place_ends(jax.random.randint(keys[3], (DEVICES, SEQ_DEV), 0, SETS), jax.random.fold_in(keys[3], 1), 0, SETS - 1).astype(jnp.int32),
        "dispatch": draw_dispatch(jax.random.fold_in(keys[22], 71), 0),
        "norm_first": jnp.clip(1.0 + 0.1 * jax.random.normal(keys[5], (D,), jnp.float32), 0.5, 1.5).astype(jnp.bfloat16),
        "norm_second": jnp.clip(1.0 + 0.1 * jax.random.normal(keys[6], (D,), jnp.float32), 0.5, 1.5).astype(jnp.bfloat16),
        "w_qkv": bell_draw(keys[7], (D, QKV), D ** -0.5, 0.15625, ((0, 8),)),
        "w_out": bell_draw(keys[8], (QWIDTH, D), (QWIDTH // 16) ** -0.5, 0.625, ((0, 8),)),
        "w_router": bell_draw(keys[9], (D, EXPERTS), (4 * D) ** -0.5, 0.078125),
        "w_gate_up": bell_draw(keys[10], (EXPERTS, D, 2 * FF), D ** -0.5, 0.15625, ((0, 8),)),
        "w_down": bell_draw(keys[11], (EXPERTS, FF, D), (FF // 4) ** -0.5, 0.375, ((0, 8),)),
        "qkv_down": bell_draw(keys[12], (SETS, D, 3 * R), D ** -0.5, 0.15625, ((0, 8),)),
        "qkv_up": bell_draw(keys[13], (SETS, R, QKV), (4 * R) ** -0.5, 0.75, ((0, 8),)),
        "out_down": bell_draw(keys[14], (SETS, QWIDTH, R), QWIDTH ** -0.5, 0.15625, ((0, 8),)),
        "out_up": bell_draw(keys[15], (SETS, R, D), (R // 4) ** -0.5, 3.0, ((0, 8),)),
        "router_down": bell_draw(keys[16], (SETS, D, R), D ** -0.5, 0.15625, ((0, 8),)),
        "router_up": bell_draw(keys[17], (SETS, R, EXPERTS), (4 * R) ** -0.5, 0.75, ((0, 8),)),
        "gu_down": bell_draw(keys[18], (EXPERTS, SETS, D, 2 * R), D ** -0.5, 0.15625, ((0, 8),)),
        "gu_up": bell_draw(keys[19], (EXPERTS, SETS, R, 2 * FF), (4 * R) ** -0.5, 0.75, ((0, 8),)),
        "dn_down": bell_draw(keys[20], (EXPERTS, SETS, FF, R), FF ** -0.5, 0.1875, ((0, 8),)),
        "dn_up": bell_draw(keys[21], (EXPERTS, SETS, R, D), R ** -0.5, 1.5, ((0, 8),)),
    }


EPS = 1e-05
HIGHEST = lax.Precision.HIGHEST

@jax.custom_vjp
def low(v):
    return lax.optimization_barrier(v.astype(jnp.bfloat16)).astype(jnp.float32)

@jax.custom_vjp
def low_back(v):
    return v

def low_keep(v):
    return (low(v), None)

def low_pass(kept, grad):
    return (grad,)

def back_keep(v):
    return (v, None)

def back_low(kept, grad):
    return (low(grad),)
low.defvjp(low_keep, low_pass)
low_back.defvjp(back_keep, back_low)

def rms_norm(values, norm_gain):
    return values * lax.rsqrt(lax.optimization_barrier(jnp.mean(values * values, axis=-1, keepdims=True)) + EPS) * norm_gain

def softmax_last(values):
    row_max = lax.optimization_barrier(jnp.max(values, axis=-1, keepdims=True))
    shifted = jnp.exp(values - row_max)
    return shifted / lax.optimization_barrier(jnp.sum(shifted, axis=-1, keepdims=True))

def adapter_in(inputs, down_all, select):
    lowered = jnp.einsum('td,sdk->tsk', inputs, down_all, precision=HIGHEST)
    return low_back(low(lowered * select[:, :, None]))

def adapter_out(lowered, up_part):
    return jnp.einsum('tsk,skn->tn', lowered, up_part, precision=HIGHEST)

def expert_in(inputs, down_all, select):
    lowered = jnp.einsum('eqd,esdk->eqsk', inputs, down_all, precision=HIGHEST)
    return low_back(low(lowered * select[..., None]))

def expert_out(lowered, up_part):
    return jnp.einsum('eqsk,eskn->eqn', lowered, up_part, precision=HIGHEST)

def routing(lengths_dev, sets_dev, dispatch_dev):
    token_rows = dispatch_dev.shape[0]
    position = jnp.arange(token_rows, dtype=jnp.int32)
    seq_ends = jnp.cumsum(lengths_dev).astype(jnp.int32)
    segment = lax.optimization_barrier(jnp.sum((position[:, None] >= seq_ends[None, :]).astype(jnp.int32), axis=1))
    seq_pick = segment[:, None] == jnp.arange(SEQ_DEV, dtype=jnp.int32)[None, :]
    token_set = lax.optimization_barrier(jnp.sum(jnp.where(seq_pick, sets_dev[None, :], 0), axis=1)).astype(jnp.int32)
    select = (token_set[:, None] == jnp.arange(SETS, dtype=jnp.int32)[None, :]).astype(jnp.float32)
    allowed = (position[None, :] <= position[:, None]) & (segment[None, :] == segment[:, None])
    slots = dispatch_dev.reshape(-1).astype(jnp.int32)
    per_expert = PEER_ROWS // EXP_DEV
    expert_of = (EXP_DEV * (slots // PEER_ROWS % N_GROUP) + slots % PEER_ROWS // per_expert).astype(jnp.int32)
    copy_index = jnp.arange(2 * token_rows, dtype=jnp.int32)
    sorted_copies = jnp.argsort(expert_of * (2 * token_rows) + copy_index).astype(jnp.int32)
    inverse = jnp.argsort(sorted_copies).astype(jnp.int32)
    tok_sorted = (sorted_copies // 2).reshape(EXPERTS, 2 * token_rows // EXPERTS)
    copy_sel = select[tok_sorted]
    chosen = (expert_of.reshape(token_rows, 2)[:, :, None] == jnp.arange(EXPERTS, dtype=jnp.int32)[None, None, :]).astype(jnp.float32)
    return (select, allowed, tok_sorted, copy_sel, inverse, chosen)

def device_block(tokens_dev, adapters, base, routing_info):
    qkv_down, qkv_up, out_down, out_up, router_down, router_up, gu_down, gu_up, dn_down, dn_up = adapters
    norm_first, norm_second, w_qkv, w_out, w_router, w_gate_up, w_down = base
    select, allowed, tok_sorted, copy_sel, inverse, chosen = routing_info
    token_rows = tokens_dev.shape[0]
    query_width = QUERY_HEADS * HEAD_SIZE
    key_value_width = KEY_VALUE_HEADS * HEAD_SIZE
    head_grouping = QUERY_HEADS // KEY_VALUE_HEADS
    normed_in = low(rms_norm(tokens_dev, norm_first))
    low_q = adapter_in(normed_in, qkv_down, select)
    extra = jnp.concatenate([adapter_out(low_q[:, :, 0:R], qkv_up[:, :, 0:query_width]), adapter_out(low_q[:, :, R:2 * R], qkv_up[:, :, query_width:query_width + key_value_width]), adapter_out(low_q[:, :, 2 * R:3 * R], qkv_up[:, :, query_width + key_value_width:])], axis=1)
    query_key_value = low_back(low(jnp.dot(normed_in, w_qkv, precision=HIGHEST) + extra))
    query_rows = query_key_value[:, :query_width].reshape(token_rows, KEY_VALUE_HEADS, head_grouping, HEAD_SIZE)
    every_key_row = query_key_value[:, query_width:query_width + key_value_width].reshape(token_rows, KEY_VALUE_HEADS, HEAD_SIZE)
    every_value_row = query_key_value[:, query_width + key_value_width:].reshape(token_rows, KEY_VALUE_HEADS, HEAD_SIZE)
    scores = low_back(jnp.einsum('tgjd,ugd->gjtu', query_rows, every_key_row, precision=HIGHEST) * HEAD_SIZE ** (-0.5))
    scores = jnp.where(allowed, scores, -1e+30)
    probs = low(softmax_last(scores))
    context = jnp.einsum('gjtu,ugd->tgjd', probs, every_value_row, precision=HIGHEST).reshape(token_rows, query_width)
    context = low_back(low(context))
    low_o = adapter_in(context, out_down, select)
    attn = low_back(jnp.dot(context, w_out, precision=HIGHEST) + adapter_out(low_o, out_up))
    middle = tokens_dev + attn
    normed_mid = low(rms_norm(middle, norm_second))
    low_r = adapter_in(normed_mid, router_down, select)
    logits = low_back(jnp.dot(normed_mid, w_router, precision=HIGHEST) + adapter_out(low_r, router_up))
    picked = lax.optimization_barrier(jnp.sum(logits[:, None, :] * chosen, axis=-1))
    gates = softmax_last(picked)
    expert_rows = low_back(normed_mid[tok_sorted])
    low_g = expert_in(expert_rows, gu_down, copy_sel)
    gate_up = jnp.einsum('eqd,edf->eqf', expert_rows, w_gate_up, precision=HIGHEST) + jnp.concatenate([expert_out(low_g[..., 0:R], gu_up[..., 0:FF]), expert_out(low_g[..., R:2 * R], gu_up[..., FF:2 * FF])], axis=2)
    gate_up = low_back(gate_up)
    gate_part = gate_up[..., :FF]
    hidden = low(gate_part / (1.0 + jnp.exp(-gate_part)) * gate_up[..., FF:])
    low_d = expert_in(hidden, dn_down, copy_sel)
    result = jnp.einsum('eqf,efd->eqd', hidden, w_down, precision=HIGHEST) + expert_out(low_d, dn_up)
    result = low_back(low(result))
    per_copy = result.reshape(2 * token_rows, D)[inverse].reshape(token_rows, 2, D)
    return middle + lax.optimization_barrier(jnp.sum(gates[:, :, None] * per_copy, axis=1))

def reference(tokens, grad_out, lengths, adapter_ids, dispatch, norm_first, norm_second, w_qkv, w_out, w_router, w_gate_up, w_down, qkv_down, qkv_up, out_down, out_up, router_down, router_up, gu_down, gu_up, dn_down, dn_up):
    base = tuple((weight.astype(jnp.float32) for weight in (norm_first, norm_second, w_qkv, w_out, w_router, w_gate_up, w_down)))
    adapters = tuple((weight.astype(jnp.float32) for weight in (qkv_down, qkv_up, out_down, out_up, router_down, router_up, gu_down, gu_up, dn_down, dn_up)))
    stacked = (tokens.reshape(DEVICES, TOK_DEV, D), grad_out.reshape(DEVICES, TOK_DEV, D), lengths, adapter_ids, dispatch.reshape(DEVICES, TOK_DEV, 2))

    def one_device(running, device_item):
        tokens_dev, grad_dev, lengths_dev, sets_dev, dispatch_dev = device_item
        routing_info = routing(lengths_dev, sets_dev, dispatch_dev)

        def forward(inputs, adapter_vals):
            return device_block(inputs, adapter_vals, base, routing_info)
        result, pullback = jax.vjp(forward, tokens_dev.astype(jnp.float32), adapters)
        grad_in, grad_adapters = pullback(grad_dev.astype(jnp.float32))
        running = jax.tree.map(lambda summed, fresh: summed + fresh, running, grad_adapters)
        return (running, (result.astype(jnp.bfloat16), grad_in))
    zeros_tree = jax.tree.map(jnp.zeros_like, adapters)
    totals, (outputs, grads_in) = lax.scan(one_device, zeros_tree, stacked)
    return (outputs.reshape(TOKENS, D), grads_in.reshape(TOKENS, D), totals[0], totals[1], totals[2], totals[3], totals[4], totals[5], totals[6], totals[7], totals[8], totals[9])
```

```python
import jax
import jax.numpy as jnp
from jax import lax
from jax.sharding import Mesh
from jax.sharding import PartitionSpec as P

QUERY_HEADS = 24
KEY_VALUE_HEADS = 8
HEAD_SIZE = 64
FF = 1024
R = 16
SETS = 8


EPS = 1e-05


def row_norm(values, norm_gain):
    inv_root = lax.rsqrt(jnp.mean(values * values, axis=-1, keepdims=True) + EPS)
    return (values * inv_root * norm_gain, inv_root)


def norm_back(upstream, values, inv_root, norm_gain):
    scaled = norm_gain * upstream
    return inv_root * scaled - values * inv_root**3 * jnp.mean(
        scaled * values, axis=-1, keepdims=True
    )


def softmax_last(values):
    row_max = jnp.max(values, axis=-1, keepdims=True)
    shifted = jnp.exp(values - row_max)
    return shifted / jnp.sum(shifted, axis=-1, keepdims=True)


def adapter_down(inputs, down_all, select):
    lowered = jnp.einsum("td,sdk->tsk", inputs, down_all, preferred_element_type=jnp.float32)
    return (lowered * select[:, :, None]).astype(jnp.bfloat16)


def adapter_up(lowered, up_all, col_spans):
    return jnp.concatenate(
        [
            jnp.einsum(
                "tsk,skn->tn",
                lowered[:, :, rank_lo:rank_hi],
                up_all[:, :, col_lo:col_hi],
                preferred_element_type=jnp.float32,
            )
            for rank_lo, rank_hi, col_lo, col_hi in col_spans
        ],
        axis=1,
    )


def adapter_back(upstream, lowered, inputs, down_all, up_all, select, col_spans):
    grad_up = jnp.concatenate(
        [
            jnp.einsum(
                "tsk,tn->skn",
                lowered[:, :, rank_lo:rank_hi],
                upstream[:, col_lo:col_hi],
                preferred_element_type=jnp.float32,
            )
            for rank_lo, rank_hi, col_lo, col_hi in col_spans
        ],
        axis=2,
    )
    grad_low = jnp.concatenate(
        [
            jnp.einsum(
                "tn,skn->tsk",
                upstream[:, col_lo:col_hi],
                up_all[:, :, col_lo:col_hi],
                preferred_element_type=jnp.float32,
            )
            for rank_lo, rank_hi, col_lo, col_hi in col_spans
        ],
        axis=2,
    )
    grad_low = (grad_low * select[:, :, None]).astype(jnp.bfloat16)
    grad_down = jnp.einsum("td,tsk->sdk", inputs, grad_low, preferred_element_type=jnp.float32)
    grad_in = jnp.einsum("tsk,sdk->td", grad_low, down_all, preferred_element_type=jnp.float32)
    return (grad_in, grad_down, grad_up)


def expert_down(inputs, down_all, select):
    lowered = jnp.einsum("nemd,esdk->nemsk", inputs, down_all, preferred_element_type=jnp.float32)
    return (lowered * select[..., None]).astype(jnp.bfloat16)


def expert_up(lowered, up_all, col_spans):
    return jnp.concatenate(
        [
            jnp.einsum(
                "nemsk,eskf->nemf",
                lowered[..., rank_lo:rank_hi],
                up_all[..., col_lo:col_hi],
                preferred_element_type=jnp.float32,
            )
            for rank_lo, rank_hi, col_lo, col_hi in col_spans
        ],
        axis=3,
    )


def expert_back(upstream, lowered, inputs, down_all, up_all, select, col_spans):
    grad_up = jnp.concatenate(
        [
            jnp.einsum(
                "nemsk,nemf->eskf",
                lowered[..., rank_lo:rank_hi],
                upstream[..., col_lo:col_hi],
                preferred_element_type=jnp.float32,
            )
            for rank_lo, rank_hi, col_lo, col_hi in col_spans
        ],
        axis=3,
    )
    grad_low = jnp.concatenate(
        [
            jnp.einsum(
                "nemf,eskf->nemsk",
                upstream[..., col_lo:col_hi],
                up_all[..., col_lo:col_hi],
                preferred_element_type=jnp.float32,
            )
            for rank_lo, rank_hi, col_lo, col_hi in col_spans
        ],
        axis=4,
    )
    grad_low = (grad_low * select[..., None]).astype(jnp.bfloat16)
    grad_down = jnp.einsum("nemd,nemsk->esdk", inputs, grad_low, preferred_element_type=jnp.float32)
    grad_in = jnp.einsum("nemsk,esdk->nemd", grad_low, down_all, preferred_element_type=jnp.float32)
    return (grad_in, grad_down, grad_up)


X_PAIRS = [(0, 1), (1, 0), (2, 3), (3, 2)]
Y_PAIRS = [(0, 2), (2, 0), (1, 3), (3, 1)]
CORE_PAIRS = [(0, 1), (1, 0)]
GROUP = ("chip", "core")


def to_wide(value):
    return value.astype(jnp.float32)


def to_low(value):
    return value.astype(jnp.bfloat16)


def scatter_group(blocks):
    chip = lax.axis_index("chip")
    core = lax.axis_index("core")
    by_core = blocks.reshape((4, 2) + blocks.shape[1:])
    mine = lax.dynamic_index_in_dim(by_core, core, 1, keepdims=False)
    other = lax.dynamic_index_in_dim(by_core, 1 - core, 1, keepdims=False)
    summed = to_low(to_wide(mine) + to_wide(lax.ppermute(other, "core", CORE_PAIRS)))
    half = blocks.shape[1] // 2
    rel = [lax.dynamic_index_in_dim(summed, chip ^ k, 0, keepdims=False) for k in range(4)]
    first = [block[:half] for block in rel]
    second = [block[half:] for block in rel]
    got_first = lax.ppermute(jnp.concatenate([first[1], first[3]]), "chip", X_PAIRS)
    got_second = lax.ppermute(jnp.concatenate([second[2], second[3]]), "chip", Y_PAIRS)
    keep_first = to_wide(first[0]) + to_wide(got_first[:half])
    send_first = to_low(to_wide(first[2]) + to_wide(got_first[half:]))
    rest = blocks.shape[1] - half
    keep_second = to_wide(second[0]) + to_wide(got_second[:rest])
    send_second = to_low(to_wide(second[1]) + to_wide(got_second[rest:]))
    last_first = lax.ppermute(send_first, "chip", Y_PAIRS)
    last_second = lax.ppermute(send_second, "chip", X_PAIRS)
    return jnp.concatenate([keep_first + to_wide(last_first), keep_second + to_wide(last_second)])


def sum_replicas(values):
    return [to_wide(lax.psum(value, "dp")) for value in values]


def to_experts(send_rows, send_sets):
    got_rows, got_sets = (
        lax.all_to_all(send_rows, GROUP, split_axis=0, concat_axis=0, tiled=True),
        lax.all_to_all(send_sets, GROUP, split_axis=0, concat_axis=0, tiled=True),
    )
    return (got_rows, got_sets)


def to_sources(send_rows):
    return lax.all_to_all(send_rows, GROUP, split_axis=0, concat_axis=0, tiled=True)


def body(
    tokens,
    grad_out,
    lengths,
    adapter_ids,
    dispatch,
    norm_first,
    norm_second,
    w_qkv,
    w_out,
    w_router,
    w_gate_up,
    w_down,
    qkv_down,
    qkv_up,
    out_down,
    out_up,
    router_down,
    router_up,
    gu_down,
    gu_up,
    dn_down,
    dn_up,
):
    token_rows, features = tokens.shape
    dp_size = lax.axis_size("dp")
    group_size = lax.axis_size("chip") * lax.axis_size("core")
    devices = group_size
    old_rows = 2 * token_rows // (dp_size * group_size)
    peer_rows = 2 * token_rows // devices
    local_experts = w_down.shape[0]
    per_expert = peer_rows // local_experts
    expert_count = w_router.shape[1]
    query_width = QUERY_HEADS * HEAD_SIZE
    key_value_width = KEY_VALUE_HEADS * HEAD_SIZE
    head_grouping = QUERY_HEADS // KEY_VALUE_HEADS
    scale = HEAD_SIZE ** (-0.5)
    position = jnp.arange(token_rows, dtype=jnp.int32)
    seq_ends = jnp.cumsum(lengths[0])
    segment = jnp.sum((position[:, None] >= seq_ends[None, :]).astype(jnp.int32), axis=1)
    seq_pick = segment[:, None] == jnp.arange(lengths.shape[1], dtype=jnp.int32)[None, :]
    token_set = jnp.sum(jnp.where(seq_pick, adapter_ids[0][None, :], 0), axis=1)
    set_range = jnp.arange(SETS, dtype=jnp.int32)
    select = (token_set[:, None] == set_range[None, :]).astype(jnp.float32)
    allowed = (position[None, :] <= position[:, None]) & (segment[None, :] == segment[:, None])
    local_slots = dispatch.reshape(-1)
    old_per_expert = old_rows // local_experts
    replica = local_slots // (group_size * old_rows)
    half_of = local_slots % old_rows // old_per_expert
    slots = (
        (local_slots // old_rows % group_size) * peer_rows
        + half_of * per_expert
        + replica * old_per_expert
        + local_slots % old_per_expert
    )
    owner = (
        jnp.zeros((2 * token_rows,), jnp.int32)
        .at[slots]
        .set(jnp.arange(2 * token_rows, dtype=jnp.int32))
    )
    source_row = owner // 2
    expert_of = local_experts * (slots // peer_rows % group_size) + slots % peer_rows // per_expert
    chosen = (
        expert_of.reshape(token_rows, 2)[:, :, None]
        == jnp.arange(expert_count, dtype=jnp.int32)[None, None, :]
    ).astype(jnp.float32)
    own_pack = jnp.concatenate(
        [
            jnp.swapaxes(qkv_down, 1, 2),
            jnp.swapaxes(out_down, 1, 2),
            jnp.swapaxes(router_down, 1, 2),
            out_up,
            jnp.pad(router_up, ((0, 0), (0, 0), (0, features - expert_count))),
        ],
        axis=1,
    )
    full_pack = lax.all_gather(own_pack, GROUP, axis=0, tiled=True)
    full_qd = jnp.swapaxes(full_pack[:, : 3 * R], 1, 2)
    full_od = jnp.swapaxes(full_pack[:, 3 * R : 4 * R], 1, 2)
    full_rd = jnp.swapaxes(full_pack[:, 4 * R : 5 * R], 1, 2)
    full_ou = full_pack[:, 5 * R : 6 * R]
    full_ru = full_pack[:, 6 * R :, :expert_count]
    full_qu = lax.all_gather(qkv_up, GROUP, axis=0, tiled=True)
    tokens_wide = tokens.astype(jnp.float32)
    gain_first = norm_first.astype(jnp.float32)
    gain_second = norm_second.astype(jnp.float32)
    normed, root_first = row_norm(tokens_wide, gain_first)
    normed_in = normed.astype(jnp.bfloat16)
    qkv_spans = [
        (0, R, 0, query_width),
        (R, 2 * R, query_width, query_width + key_value_width),
        (2 * R, 3 * R, query_width + key_value_width, query_width + 2 * key_value_width),
    ]
    low_q = adapter_down(normed_in, full_qd, select)
    columns = normed_in
    qkv_base = jnp.dot(
        columns,
        lax.all_gather(w_qkv, GROUP, axis=0, tiled=True),
        preferred_element_type=jnp.float32,
    )
    query_key_value = (qkv_base + adapter_up(low_q, full_qu, qkv_spans)).astype(jnp.bfloat16)
    query_rows = query_key_value[:, :query_width].reshape(
        token_rows, KEY_VALUE_HEADS, head_grouping, HEAD_SIZE
    )
    every_key_row = query_key_value[:, query_width : query_width + key_value_width].reshape(
        token_rows, KEY_VALUE_HEADS, HEAD_SIZE
    )
    every_value_row = query_key_value[:, query_width + key_value_width :].reshape(
        token_rows, KEY_VALUE_HEADS, HEAD_SIZE
    )

    def attend_scores():
        raw_scores = (
            jnp.einsum(
                "tgjd,ugd->gjtu", query_rows, every_key_row, preferred_element_type=jnp.float32
            )
            * scale
        )
        return jnp.where(allowed, raw_scores, -1e30)

    scores = attend_scores()
    row_max = jnp.max(scores, axis=-1, keepdims=True)
    log_total = row_max + jnp.log(jnp.sum(jnp.exp(scores - row_max), axis=-1, keepdims=True))
    probs_low = jnp.exp(scores - log_total).astype(jnp.bfloat16)
    context = (
        jnp.einsum("gjtu,ugd->tgjd", probs_low, every_value_row, preferred_element_type=jnp.float32)
        .reshape(token_rows, query_width)
        .astype(jnp.bfloat16)
    )
    whole_width = [(0, R, 0, features)]
    low_o = adapter_down(context, full_od, select)
    columns = context
    attn_base = jnp.dot(
        columns,
        lax.all_gather(w_out, GROUP, axis=0, tiled=True),
        preferred_element_type=jnp.float32,
    )
    middle = tokens_wide + (attn_base + adapter_up(low_o, full_ou, whole_width))
    normed_two, root_second = row_norm(middle, gain_second)
    normed_mid = normed_two.astype(jnp.bfloat16)
    router_spans = [(0, R, 0, expert_count)]
    low_r = adapter_down(normed_mid, full_rd, select)
    logits = jnp.dot(normed_mid, w_router, preferred_element_type=jnp.float32) + adapter_up(
        low_r, full_ru, router_spans
    )
    picked = jnp.sum(logits[:, None, :] * chosen, axis=-1)
    gates = softmax_last(picked)
    send_rows = normed_mid[source_row].reshape(devices, peer_rows, features)
    send_sets = token_set[source_row].reshape(devices, peer_rows)
    got_rows, got_sets = to_experts(send_rows, send_sets)
    expert_in = got_rows.reshape(devices, local_experts, per_expert, features)
    expert_sel = (
        got_sets.reshape(devices, local_experts, per_expert)[..., None] == set_range
    ).astype(jnp.float32)
    gu_spans = [(0, R, 0, FF), (R, 2 * R, FF, 2 * FF)]
    low_g = expert_down(expert_in, gu_down, expert_sel)
    gate_up = jnp.einsum(
        "nemd,edf->nemf", expert_in, w_gate_up, preferred_element_type=jnp.float32
    ) + expert_up(low_g, gu_up, gu_spans)
    gate_part = gate_up[..., :FF]
    up_part = gate_up[..., FF:]
    sigmoid_gate = 1.0 / (1.0 + jnp.exp(-gate_part))
    hidden = (gate_part * sigmoid_gate * up_part).astype(jnp.bfloat16)
    low_d = expert_down(hidden, dn_down, expert_sel)
    expert_out = (
        jnp.einsum("nemf,efd->nemd", hidden, w_down, preferred_element_type=jnp.float32)
        + expert_up(low_d, dn_up, whole_width)
    ).astype(jnp.bfloat16)
    returned = to_sources(expert_out.reshape(devices, peer_rows, features))
    per_copy = (
        returned.reshape(2 * token_rows, features)[slots]
        .reshape(token_rows, 2, features)
        .astype(jnp.float32)
    )
    block_out = middle + jnp.sum(gates[:, :, None] * per_copy, axis=1)
    upstream = grad_out.astype(jnp.float32)
    grad_gates = jnp.sum(upstream[:, None, :] * per_copy, axis=-1)
    grad_copy = (gates[:, :, None] * upstream[:, None, :]).astype(jnp.bfloat16)
    send_grad = grad_copy.reshape(2 * token_rows, features)[owner].reshape(
        devices, peer_rows, features
    )
    got_grad, sets_back = to_experts(send_grad, send_sets)
    grad_result = got_grad.reshape(devices, local_experts, per_expert, features)
    sel_back = (
        sets_back.reshape(devices, local_experts, per_expert)[..., None] == set_range
    ).astype(jnp.float32)
    grad_hidden = jnp.einsum(
        "nemd,efd->nemf", grad_result, w_down, preferred_element_type=jnp.float32
    )
    hidden_extra, grad_dn_down, grad_dn_up = expert_back(
        grad_result, low_d, hidden, dn_down, dn_up, sel_back, whole_width
    )
    grad_hidden = grad_hidden + hidden_extra
    grad_gate = grad_hidden * up_part * sigmoid_gate * (1.0 + gate_part * (1.0 - sigmoid_gate))
    grad_upper = grad_hidden * gate_part * sigmoid_gate
    grad_gu = jnp.concatenate([grad_gate, grad_upper], axis=3).astype(jnp.bfloat16)
    grad_rows = jnp.einsum("nemf,edf->nemd", grad_gu, w_gate_up, preferred_element_type=jnp.float32)
    rows_extra, grad_gu_down, grad_gu_up = expert_back(
        grad_gu, low_g, expert_in, gu_down, gu_up, sel_back, gu_spans
    )
    grad_rows = (grad_rows + rows_extra).astype(jnp.bfloat16)
    came_back = to_sources(grad_rows.reshape(devices, peer_rows, features))
    grad_mid_norm = jnp.sum(
        came_back.reshape(2 * token_rows, features)[slots]
        .reshape(token_rows, 2, features)
        .astype(jnp.float32),
        axis=1,
    )
    grad_pick = gates * (grad_gates - jnp.sum(gates * grad_gates, axis=-1, keepdims=True))
    grad_logits = jnp.sum(grad_pick[:, :, None] * chosen, axis=1).astype(jnp.bfloat16)
    grad_mid_norm = grad_mid_norm + jnp.einsum(
        "te,de->td", grad_logits, w_router, preferred_element_type=jnp.float32
    )
    router_extra, grad_rd, grad_ru = adapter_back(
        grad_logits, low_r, normed_mid, full_rd, full_ru, select, router_spans
    )
    grad_mid_norm = grad_mid_norm + router_extra
    grad_middle = upstream + norm_back(grad_mid_norm, middle, root_second, gain_second)
    grad_attn = grad_middle.astype(jnp.bfloat16)
    context_gradient = jnp.einsum(
        "td,cd->tc",
        grad_attn,
        lax.all_gather(w_out, GROUP, axis=0, tiled=True),
        preferred_element_type=jnp.float32,
    )
    context_extra, grad_od, grad_ou = adapter_back(
        grad_attn, low_o, context, full_od, full_ou, select, whole_width
    )
    context_gradient = (context_gradient + context_extra).astype(jnp.bfloat16)
    head_gradients = context_gradient.reshape(token_rows, KEY_VALUE_HEADS, head_grouping, HEAD_SIZE)
    probs_again = jnp.exp(attend_scores() - log_total)
    grad_probs = jnp.einsum(
        "tgjd,ugd->gjtu", head_gradients, every_value_row, preferred_element_type=jnp.float32
    )
    row_delta = jnp.sum(probs_again * grad_probs, axis=-1, keepdims=True)
    grad_scores = (probs_again * (grad_probs - row_delta)).astype(jnp.bfloat16)
    grad_query = (
        jnp.einsum("gjtu,ugd->tgjd", grad_scores, every_key_row, preferred_element_type=jnp.float32)
        * scale
    )
    grad_keys = (
        jnp.einsum("gjtu,tgjd->ugd", grad_scores, query_rows, preferred_element_type=jnp.float32)
        * scale
    )
    grad_values = jnp.einsum(
        "gjtu,tgjd->ugd",
        probs_again.astype(jnp.bfloat16),
        head_gradients,
        preferred_element_type=jnp.float32,
    )
    grad_qkv = jnp.concatenate(
        [
            grad_query.reshape(token_rows, query_width),
            grad_keys.reshape(token_rows, key_value_width),
            grad_values.reshape(token_rows, key_value_width),
        ],
        axis=1,
    ).astype(jnp.bfloat16)
    grad_normed = jnp.einsum(
        "tc,dc->td",
        grad_qkv,
        lax.all_gather(w_qkv, GROUP, axis=0, tiled=True),
        preferred_element_type=jnp.float32,
    )
    normed_extra, grad_qd, grad_qu = adapter_back(
        grad_qkv, low_q, normed_in, full_qd, full_qu, select, qkv_spans
    )
    grad_tokens = grad_middle + norm_back(
        grad_normed + normed_extra, tokens_wide, root_first, gain_first
    )
    packed = jnp.concatenate(
        [
            to_low(jnp.swapaxes(grad_qd, 1, 2)),
            to_low(jnp.swapaxes(grad_od, 1, 2)),
            to_low(jnp.swapaxes(grad_rd, 1, 2)),
            to_low(grad_ou),
            jnp.pad(to_low(grad_ru), ((0, 0), (0, 0), (0, features - expert_count))),
        ],
        axis=1,
    )
    experts = sum_replicas(
        [
            to_low(jnp.swapaxes(grad_gu_down, 2, 3)),
            to_low(grad_gu_up),
            to_low(jnp.swapaxes(grad_dn_down, 2, 3)),
            to_low(grad_dn_up),
        ]
    )
    share, share_up = scatter_group(packed), scatter_group(to_low(grad_qu))
    share, share_up, experts = lax.optimization_barrier((share, share_up, experts))
    own_packed, own_up = sum_replicas([to_low(share), to_low(share_up)])
    totals = (
        jnp.swapaxes(own_packed[None, : 3 * R], 1, 2),
        own_up[None],
        jnp.swapaxes(own_packed[None, 3 * R : 4 * R], 1, 2),
        own_packed[None, 5 * R : 6 * R],
        jnp.swapaxes(own_packed[None, 4 * R : 5 * R], 1, 2),
        own_packed[None, 6 * R :, :expert_count],
        jnp.swapaxes(experts[0], 2, 3),
        experts[1],
        jnp.swapaxes(experts[2], 2, 3),
        experts[3],
    )
    return (
        block_out.astype(jnp.bfloat16),
        grad_tokens,
        totals[0],
        totals[1],
        totals[2],
        totals[3],
        totals[4],
        totals[5],
        totals[6],
        totals[7],
        totals[8],
        totals[9],
    )


def solution(mesh):
    devices = mesh.devices
    chips = devices.shape[1] // 2
    mesh = Mesh(devices.reshape(devices.shape[0], chips, 2), ("dp", "chip", "core"))
    rows = P(("dp", "chip", "core"), None)

    def over(rank):
        return P(("chip", "core"), *([None] * (rank - 1)))

    return jax.shard_map(
        body,
        mesh=mesh,
        in_specs=(
            rows,
            rows,
            rows,
            rows,
            rows,
            P(),
            P(),
            over(2),
            over(2),
            P(),
            over(3),
            over(3),
            over(3),
            over(3),
            over(3),
            over(3),
            over(3),
            over(3),
            over(4),
            over(4),
            over(4),
            over(4),
        ),
        out_specs=(
            rows,
            rows,
            over(3),
            over(3),
            over(3),
            over(3),
            over(3),
            over(3),
            over(4),
            over(4),
            over(4),
            over(4),
        ),
        check_vma=False,
    )
```
